32 devices in a mesh: rows: 8 (over y, x, core), cols: 4 (over z).
Axes of the slice: x: 2, y: 2, z: 4, core: 2. Of those that a mesh axis runs over, the one named last changes fastest.
Arguments:
- feats: bfloat16 [32768, 512], P('rows', 'cols'), may hold values from -6 to 6
- adj_vals: bfloat16 [256, 16, 128, 128], P('rows'), may hold values from -0.125 to 0.125
- colref: int32 [256, 16], P('rows'), may hold values from 0 to 47, as said below
- fetch_ids: int32 [8, 8, 2], P('rows'), may hold values from -1 to 31, as said below
- w_self: bfloat16 [512, 512], replicated, may hold values from -0.25 to 0.25
- w_neigh: bfloat16 [512, 512], replicated, may hold values from -0.25 to 0.25
- grad_out: bfloat16 [32768, 512], P(('rows', 'cols')), may hold values from -6 to 6
Outputs:
- act_out: bfloat16 [32768, 512], P(('rows', 'cols'))
- grad_self_w: float32 [512, 512], replicated
- grad_neigh_w: float32 [512, 512], replicated
- grad_feats: float32 [32768, 512], P('rows', 'cols')
The draws below stay inside these ranges and needn't reach their ends.
Inputs may be any that keep to these rules, and one draw needn't show every extreme that they name: `fetch_ids`: entry [r, o, s] is a row tile index within partition o (0 to 31) that partition r reads, or -1 for an empty slot. The entries of one r and o are distinct, all slots with o = r are empty, and every r fills all 2 slots of at least one o. `colref`: entry [b, k], with r = b // 32, is below 32 for partition r's own row tile of that index, or 32 + o * 2 + s for the slot s of fetch_ids[r, o], never an empty slot; so it lies in 0 to 32 + 8 * 2 - 1. The 16 entries of a row tile are distinct and the first is b - r * 32, the row tile itself.
All inputs are finite; a program needn't handle non-finite values.
Results may differ from the reference program's by a relative error of at most 0.0057.
Values may be sent and summed in bfloat16 or wider, within the bound.
No kernel may reach another device: no remote copies, remote signals or barrier semaphores. Data moves between devices by JAX's collectives and lax.ppermute only.
A program may use at most 192 MiB of HBM per device.

```python
import math
import jax
import jax.numpy as jnp
from jax import lax

HID = 512
TILE = 128
RB = 32
K = 16
CAP = 2
NODES = 32768
NBLOCKS = 256
N_ROWS = 8


def draw_plan(key):
    base = jax.random.fold_in(key, 11)
    key_live, key_full, key_pick, key_refs = jax.random.split(base, 4)
    partitions = N_ROWS
    reader = jnp.arange(partitions, dtype=jnp.int32)[:, None]
    owner_part = jnp.arange(partitions, dtype=jnp.int32)[None, :]
    live_count = jax.random.randint(key_live, (partitions, partitions), 1, CAP + 1, dtype=jnp.int32)
    full_pick = jax.random.randint(key_full, (partitions, 1), 0, partitions - 1, dtype=jnp.int32)
    full_owner = (reader + 1 + full_pick) % partitions
    live_count = jnp.where(owner_part == full_owner, CAP, live_count)
    live_count = jnp.where(owner_part == reader, 0, live_count)
    scores = jax.random.randint(key_pick, (partitions, partitions, RB), 0, 2 ** 20, dtype=jnp.int32) * RB + jnp.arange(RB, dtype=jnp.int32)
    ordering = jnp.argsort(scores, axis=-1, stable=True)[:, :, :CAP].astype(jnp.int32)
    slot_index = jnp.arange(CAP, dtype=jnp.int32)
    fetch_table = jnp.where(slot_index[None, None, :] < live_count[:, :, None], ordering, -1).astype(jnp.int32)
    pool_size = RB + partitions * CAP
    alive_slots = jnp.concatenate([jnp.ones((partitions, RB), jnp.int32), (fetch_table >= 0).astype(jnp.int32).reshape(partitions, partitions * CAP)], axis=1)
    ref_scores = jax.random.randint(key_refs, (partitions, RB, pool_size), 0, 2 ** 16, dtype=jnp.int32) * pool_size + jnp.arange(pool_size, dtype=jnp.int32)
    ref_scores = jnp.where(alive_slots[:, None, :] > 0, ref_scores, ref_scores + 2 ** 28)
    diagonal = jnp.arange(RB, dtype=jnp.int32)[:, None] == jnp.arange(pool_size, dtype=jnp.int32)[None, :]
    ref_scores = jnp.where(diagonal[None, :, :], -1, ref_scores)
    chosen = jnp.argsort(ref_scores, axis=-1, stable=True)[:, :, :K].astype(jnp.int32)
    return (fetch_table, chosen.reshape(partitions * RB, K))


def draw_colref(key, part):
    return draw_plan(key)[1]


def draw_fetch_ids(key, part):
    return draw_plan(key)[0]


def shard_levels(rng, extent, pieces, low, top_value):
    factor_of = 1.0
    for position, parts in pieces:
        steps = jax.random.uniform(jax.random.fold_in(jax.random.fold_in(rng, 6), position), (parts,), jnp.float32, low / len(pieces), top_value / len(pieces))
        factor_of = factor_of * jnp.repeat(jnp.exp(steps), extent[position] // parts).reshape((-1,) + (1,) * (len(extent) - 1 - position))
    return factor_of


def bell_draw(rng, dims, deviation, limit, cuts=(), kind=jnp.bfloat16):
    gain = shard_levels(rng, dims, cuts, -0.22, 0.18) if cuts else 1.0
    drawn = jax.random.normal(rng, dims, jnp.float32) * deviation * gain
    return jnp.minimum(jnp.maximum(drawn, -limit), limit).astype(kind)


def setup_inputs(seed: int = 0) -> dict:
    key_list = jax.random.split(jax.random.key(seed), 8)
    feats = bell_draw(key_list[0], (NODES, HID), 1.0, 6.0, ((0, 8), (1, 4)))
    adj_vals = bell_draw(key_list[1], (NBLOCKS, K, TILE, TILE), (K * TILE) ** -0.5, 0.125, ((0, 8),))
    colref = draw_colref(jax.random.fold_in(key_list[7], 71), 0)
    fetch_ids = draw_fetch_ids(jax.random.fold_in(key_list[7], 71), 0)
    w_self = bell_draw(key_list[4], (HID, HID), HID ** -0.5, 0.25)
    w_neigh = bell_draw(key_list[5], (HID, HID), HID ** -0.5, 0.25)
    grad_out = bell_draw(key_list[6], (NODES, HID), 1.0, 6.0, ((0, 32),))
    return {"feats": feats, "adj_vals": adj_vals, "colref": colref, "fetch_ids": fetch_ids, "w_self": w_self, "w_neigh": w_neigh, "grad_out": grad_out}


def tile_ids(colref, fetch_ids):
    count = colref.shape[0]
    reader = (jnp.arange(count, dtype=jnp.int32) // RB)[:, None]
    remote = jnp.maximum(colref - RB, 0).astype(jnp.int32)
    owner_part = remote // CAP
    slot_index = remote % CAP
    looked = fetch_ids[reader, owner_part, slot_index]
    return jnp.where(colref < RB, reader * RB + colref, owner_part * RB + looked).astype(jnp.int32)

def reference(feats, adj_vals, colref, fetch_ids, w_self, w_neigh, grad_out):
    all_tiles = feats.reshape(N_ROWS * RB, TILE, HID)
    tile_index = tile_ids(colref, fetch_ids).reshape(N_ROWS, RB, K)
    tile_vals = adj_vals.reshape(N_ROWS, RB, K, TILE, TILE)

    def aggregate(item_pair):
        index_set, values = item_pair
        picked = all_tiles[index_set]
        summed = jnp.einsum('bkij,bkjf->bif', values.astype(jnp.float32), picked.astype(jnp.float32))
        return summed.astype(jnp.bfloat16)
    aggregated = lax.map(aggregate, (tile_index, tile_vals)).reshape(NODES, HID)
    preact = jnp.dot(feats, w_self, preferred_element_type=jnp.float32) + jnp.dot(aggregated, w_neigh, preferred_element_type=jnp.float32)
    activation, pull_back = jax.vjp(jax.nn.gelu, preact)
    grad_pre = pull_back(grad_out.astype(jnp.float32))[0].astype(jnp.bfloat16)
    grad_scale = 1.0 / math.sqrt(NODES)
    contract = (((0,), (0,)), ((), ()))
    grad_self_w = lax.dot_general(feats, grad_pre, contract, preferred_element_type=jnp.float32) * grad_scale
    grad_neigh_w = lax.dot_general(aggregated, grad_pre, contract, preferred_element_type=jnp.float32) * grad_scale
    dims_back = (((1,), (1,)), ((), ()))
    self_part = lax.dot_general(grad_pre, w_self, dims_back, preferred_element_type=jnp.float32).astype(jnp.bfloat16)
    grad_agg = lax.dot_general(grad_pre, w_neigh, dims_back, preferred_element_type=jnp.float32).astype(jnp.bfloat16)
    grad_tiles = grad_agg.reshape(N_ROWS, RB, TILE, HID)

    def spread(running, item_set):
        index_set, values, grad_rows = item_set
        per_ref = jnp.einsum('bkij,bif->bkjf', values.astype(jnp.float32), grad_rows.astype(jnp.float32))
        pooled = jnp.zeros((N_ROWS * RB, TILE, HID), jnp.float32).at[index_set.reshape(-1)].add(per_ref.reshape(RB * K, TILE, HID))
        rounded = lax.optimization_barrier(pooled.astype(jnp.bfloat16))
        return (running + rounded.astype(jnp.float32), None)
    start_sum = jnp.zeros((N_ROWS * RB, TILE, HID), jnp.float32)
    summed_back, _ = lax.scan(spread, start_sum, (tile_index, tile_vals, grad_tiles))
    grad_feats = self_part.astype(jnp.float32) + summed_back.reshape(NODES, HID)
    return (activation.astype(jnp.bfloat16), grad_self_w, grad_neigh_w, grad_feats)
```

```python
import math

import jax
import jax.numpy as jnp
from jax import lax
from jax.experimental import pallas as pl
from jax.experimental.pallas import tpu as pltpu
from jax.sharding import PartitionSpec as P


BF16, F32 = jnp.bfloat16, jnp.float32
CHUNKS = 2
VMEM_LIMIT = 56 * 1024 * 1024


def params(dims):
    return pltpu.CompilerParams(
        dimension_semantics=("arbitrary",) * dims, vmem_limit_bytes=VMEM_LIMIT
    )


def full(shape):
    return pl.BlockSpec(shape, lambda *_: (0,) * len(shape))


def rows_at(index, tile):
    return pl.ds(pl.multiple_of(index * tile, tile), tile)


def select_tiles(wanted, feats, tile):
    slots, width = wanted.shape[0], feats.shape[1]

    def kernel(wanted_ref, feats_ref, out_ref):
        for slot in range(slots):
            source = jnp.maximum(wanted_ref[slot], 0)
            out_ref[slot * tile : (slot + 1) * tile, :] = feats_ref[rows_at(source, tile), :]

    return pl.pallas_call(
        kernel,
        out_shape=jax.ShapeDtypeStruct((slots * tile, width), feats.dtype),
        grid_spec=pltpu.PrefetchScalarGridSpec(
            num_scalar_prefetch=1,
            grid=(1,),
            in_specs=[full(feats.shape)],
            out_specs=full((slots * tile, width)),
        ),
        compiler_params=params(1),
        name="select_tiles",
    )(wanted, feats)


def aggregate(col, colref, feats, arrived, adj, chunk, parts):
    blocks, per_block, tile, _ = adj.shape
    width = feats.shape[1]
    own = feats.shape[0]
    per_part = blocks // parts
    per_chunk = per_part // CHUNKS
    chunk_rows = per_chunk * tile

    def tile_of(k, t, col_ref):
        return (k ^ col_ref[0]) * per_part + chunk * per_chunk + t

    def kernel(col_ref, colref_ref, feats_ref, arrived_ref, *refs):
        adj_refs, outs, pool = refs[:parts], refs[parts : 2 * parts], refs[-1]
        t = pl.program_id(0)

        @pl.when(t == 0)
        def _():
            pool[:own, :] = feats_ref[...]
            pool[own:, :] = arrived_ref[...]

        for k in range(parts):
            b = tile_of(k, t, col_ref)
            right = jnp.concatenate(
                [pool[rows_at(colref_ref[b, q], tile), :] for q in range(per_block)], axis=0
            )
            left = jnp.concatenate([adj_refs[k][0, q] for q in range(per_block)], axis=1)
            outs[k][...] = jnp.dot(left, right, preferred_element_type=F32).astype(BF16)

    def adj_spec(k):
        return pl.BlockSpec(
            (1, per_block, tile, tile), lambda t, c, r: (tile_of(k, t, c), 0, 0, 0)
        )

    return pl.pallas_call(
        kernel,
        out_shape=[jax.ShapeDtypeStruct((chunk_rows, width), BF16)] * parts,
        grid_spec=pltpu.PrefetchScalarGridSpec(
            num_scalar_prefetch=2,
            grid=(per_chunk,),
            in_specs=[full(feats.shape), full(arrived.shape)]
            + [adj_spec(k) for k in range(parts)],
            out_specs=[pl.BlockSpec((tile, width), lambda t, c, r: (t, 0))] * parts,
            scratch_shapes=[pltpu.VMEM((own + arrived.shape[0], width), BF16)],
        ),
        compiler_params=params(1),
        name="aggregate",
    )(col, colref, feats, arrived, *[adj] * parts)


def permuted(w_ref, col_ref, parts, width):
    return jnp.concatenate(
        [w_ref[rows_at(k ^ col_ref[0], width), :] for k in range(parts)], axis=0
    )


NT = (((1,), (1,)), ((), ()))
TN = (((0,), (0,)), ((), ()))


def dense(col, feat_parts, agg_parts, w_self, w_neigh, grad_out, act_prev, chunk):
    parts = len(feat_parts)
    chunk_rows, width = agg_parts[0].shape
    hidden = w_self.shape[1]
    steps = 2
    rows = chunk_rows // steps
    root = math.sqrt(2.0 / math.pi)

    def kernel(col_ref, *refs):
        f_refs, a_refs = refs[:parts], refs[parts : 2 * parts]
        ws_ref, wn_ref, go_ref = refs[2 * parts : 2 * parts + 3]
        outs = refs[2 * parts + 3 + (act_prev is not None) :]
        act_ref, g_ref, back = outs[0], outs[1], outs[2:]
        ws = permuted(ws_ref, col_ref, parts, width)
        wn = permuted(wn_ref, col_ref, parts, width)
        f = jnp.concatenate([r[...] for r in f_refs], axis=1)
        a = jnp.concatenate([r[...] for r in a_refs], axis=1)
        v = jnp.dot(f, ws, preferred_element_type=F32) + jnp.dot(a, wn, preferred_element_type=F32)
        square = v * v
        tanh = jnp.tanh(root * (v + 0.044715 * (square * v)))
        half = 0.5 * (1.0 + tanh)
        act_ref[...] = (v * half).astype(BF16)
        slope = half + 0.5 * v * (1.0 - tanh * tanh) * (root * (1.0 + 3 * 0.044715 * square))
        g = (go_ref[...].astype(F32) * slope).astype(BF16)
        g_ref[...] = g
        spread = lax.dot_general(g, wn, NT, preferred_element_type=F32).astype(BF16)
        for k, out in enumerate(back):
            out[...] = spread[:, k * width : (k + 1) * width]

    offset = chunk * steps
    in_specs = (
        [pl.BlockSpec((rows, width), lambda i, c: (offset + i, 0))] * parts
        + [pl.BlockSpec((rows, width), lambda i, c: (i, 0))] * parts
        + [full(w_self.shape), full(w_neigh.shape)]
        + [pl.BlockSpec((rows, hidden), lambda i, c: (offset + i, 0))]
    )
    args = [col, *feat_parts, *agg_parts, w_self, w_neigh, grad_out]
    aliases = {}
    if act_prev is not None:
        in_specs.append(pl.BlockSpec(memory_space=pl.ANY))
        aliases = {len(args): 0}
        args.append(act_prev)
    return pl.pallas_call(
        kernel,
        out_shape=[
            jax.ShapeDtypeStruct((chunk_rows * CHUNKS, hidden), BF16),
            jax.ShapeDtypeStruct((chunk_rows, hidden), BF16),
        ]
        + [jax.ShapeDtypeStruct((chunk_rows, width), BF16)] * parts,
        grid_spec=pltpu.PrefetchScalarGridSpec(
            num_scalar_prefetch=1,
            grid=(steps,),
            in_specs=in_specs,
            out_specs=[
                pl.BlockSpec((rows, hidden), lambda i, c: (offset + i, 0)),
                pl.BlockSpec((rows, hidden), lambda i, c: (i, 0)),
            ]
            + [pl.BlockSpec((rows, width), lambda i, c: (i, 0))] * parts,
        ),
        input_output_aliases=aliases,
        compiler_params=params(1),
        name="dense",
    )(*args)


def weights(col, feat_parts, agg_chunks, grads, w_self):
    parts = len(feat_parts)
    rows, width = feat_parts[0].shape
    hidden = w_self.shape[1]

    def kernel(col_ref, *refs):
        f_refs = refs[:parts]
        a_refs = refs[parts : parts + parts * CHUNKS]
        g_refs = refs[parts + parts * CHUNKS : parts + parts * CHUNKS + CHUNKS]
        ws_ref = refs[parts + parts * CHUNKS + CHUNKS]
        outs = refs[parts + parts * CHUNKS + CHUNKS + 1 :]
        wg_ref, s_refs = outs[0], outs[1:]
        g = jnp.concatenate([r[...] for r in g_refs], axis=0)
        ws = permuted(ws_ref, col_ref, parts, width)
        s = lax.dot_general(g, ws, NT, preferred_element_type=F32).astype(BF16)
        for k, out in enumerate(s_refs):
            out[...] = s[:, k * width : (k + 1) * width]
        for k in range(parts):
            at = k ^ col_ref[0]
            wg_ref[rows_at(at, width), :] = lax.dot_general(
                f_refs[k][...], g, TN, preferred_element_type=F32
            )
            a = jnp.concatenate([a_refs[h * parts + k][...] for h in range(CHUNKS)], axis=0)
            wg_ref[rows_at(at + parts, width), :] = lax.dot_general(
                a, g, TN, preferred_element_type=F32
            )

    args = [*feat_parts, *[a for chunk in agg_chunks for a in chunk], *grads, w_self]
    out_shape = [jax.ShapeDtypeStruct((2 * parts * width, hidden), F32)] + [
        jax.ShapeDtypeStruct((rows, width), BF16)
    ] * parts
    return pl.pallas_call(
        kernel,
        out_shape=out_shape,
        grid_spec=pltpu.PrefetchScalarGridSpec(
            num_scalar_prefetch=1,
            grid=(1,),
            in_specs=[full(a.shape) for a in args],
            out_specs=[full(o.shape) for o in out_shape],
        ),
        compiler_params=params(1),
        name="weights",
    )(col, *args)


def pull(col, colref, grad_chunks, adj, slots):
    blocks, per_block, tile, _ = adj.shape
    parts = len(grad_chunks[0])
    chunk_rows, width = grad_chunks[0][0].shape
    per_part = blocks // parts
    pool = blocks + slots

    def kernel(col_ref, colref_ref, *refs):
        g_refs = refs[: parts * CHUNKS]
        adj_refs = refs[parts * CHUNKS : parts * CHUNKS + parts]
        local_ref, remote_ref, grads, acc = refs[parts * CHUNKS + parts :]
        t = pl.program_id(0)

        @pl.when(t == 0)
        def _():
            acc[...] = jnp.zeros_like(acc)
            for j in range(parts):
                for h in range(CHUNKS):
                    at = (j * CHUNKS + h) * chunk_rows
                    grads[at : at + chunk_rows, :] = g_refs[h * parts + j][...]

        for k in range(parts):
            b = (k ^ col_ref[0]) * per_part + t
            turned = grads[rows_at(k * per_part + t, tile), :].T
            for q in range(0, per_block, 2):
                pair = jnp.concatenate([adj_refs[k][0, q], adj_refs[k][0, q + 1]], axis=1)
                both = jnp.dot(turned, pair, preferred_element_type=F32)
                acc[colref_ref[b, q]] += both[:, :tile]
                acc[colref_ref[b, q + 1]] += both[:, tile:]

        @pl.when(t == per_part - 1)
        def _():
            for s in range(blocks):
                local_ref[s * tile : (s + 1) * tile, :] = acc[s].T.astype(BF16)
            for s in range(slots):
                remote_ref[s * tile : (s + 1) * tile, :] = acc[blocks + s].T.astype(BF16)

    def adj_spec(k):
        return pl.BlockSpec(
            (1, per_block, tile, tile), lambda t, c, r: ((k ^ c[0]) * per_part + t, 0, 0, 0)
        )

    flat = [g for chunk in grad_chunks for g in chunk]
    return pl.pallas_call(
        kernel,
        out_shape=[
            jax.ShapeDtypeStruct((blocks * tile, width), BF16),
            jax.ShapeDtypeStruct((slots * tile, width), BF16),
        ],
        grid_spec=pltpu.PrefetchScalarGridSpec(
            num_scalar_prefetch=2,
            grid=(per_part,),
            in_specs=[full(g.shape) for g in flat] + [adj_spec(k) for k in range(parts)],
            out_specs=[full((blocks * tile, width)), full((slots * tile, width))],
            scratch_shapes=[
                pltpu.VMEM((blocks * tile, width), BF16),
                pltpu.VMEM((pool, width, tile), F32),
            ],
        ),
        compiler_params=params(1),
        name="pull",
    )(col, colref, *flat, *[adj] * parts)


def finish(col, wanted, self_parts, local, returned, tile):
    parts = len(self_parts)
    rows, _ = self_parts[0].shape
    slots = wanted.shape[0]

    def kernel(col_ref, wanted_ref, *refs):
        s_refs = refs[:parts]
        local_ref, returned_ref, out_ref = refs[parts:]
        for k in range(parts):
            at = rows_at(k ^ col_ref[0], rows)
            out_ref[at, :] = s_refs[k][...].astype(F32) + local_ref[at, :].astype(F32)
        for s in range(slots):
            target = wanted_ref[s]

            @pl.when(target >= 0)
            def _():
                out_ref[rows_at(target, tile), :] += returned_ref[
                    s * tile : (s + 1) * tile, :
                ].astype(F32)

    args = [*self_parts, local, returned]
    return pl.pallas_call(
        kernel,
        out_shape=jax.ShapeDtypeStruct(local.shape, F32),
        grid_spec=pltpu.PrefetchScalarGridSpec(
            num_scalar_prefetch=2,
            grid=(1,),
            in_specs=[full(a.shape) for a in args],
            out_specs=full(local.shape),
        ),
        compiler_params=params(1),
        name="finish",
    )(col, wanted, *args)


def swap(x, axis, k):
    n = lax.axis_size(axis)
    return lax.ppermute(x, axis, [(i, i ^ k) for i in range(n)])


def exchange(pieces, axis):
    out = [pieces[0]]
    for k in range(1, len(pieces)):
        out.append(swap(pieces[k], axis, k))
    return out


def across_rows(x):
    return lax.all_to_all(x, "rows", split_axis=0, concat_axis=0, tiled=True)


def body(feats, adj_vals, colref, fetch_ids, w_self, w_neigh, grad_out):
    node_rows, width = feats.shape
    _, _, tile, _ = adj_vals.shape
    partitions = lax.axis_size("rows")
    parts = lax.axis_size("cols")
    slots = partitions * fetch_ids.shape[2]
    total_nodes = node_rows * partitions
    c = lax.axis_index("cols")
    col = c.astype(jnp.int32).reshape(1)
    part_rows = node_rows // parts

    feat_parts = exchange(
        [lax.dynamic_slice_in_dim(feats, (c ^ k) * part_rows, part_rows) for k in range(parts)],
        "cols",
    )
    wanted = across_rows(fetch_ids.reshape(partitions, -1)).reshape(slots)
    outgoing = select_tiles(wanted, feats, tile).reshape(partitions, -1, width)
    arrived = across_rows(outgoing).reshape(slots * tile, width)

    agg_chunks = []
    for h in range(CHUNKS):
        pieces = aggregate(col, colref, feats, arrived, adj_vals, h, parts)
        agg_chunks.append(exchange(pieces, "cols"))
    act, grads, grad_chunks = None, [], []
    for h in range(CHUNKS):
        act, g, *back = dense(
            col, feat_parts, agg_chunks[h], w_self, w_neigh, grad_out, act, h
        )
        grads.append(g)
        grad_chunks.append(exchange(back, "cols"))
    partial, *self_rows = weights(col, feat_parts, agg_chunks, grads, w_self)
    self_parts = exchange(self_rows, "cols")

    hidden = w_self.shape[1]
    piece = across_rows(partial.reshape(partitions, -1, hidden)).sum(0)
    sub = piece.shape[0] // parts
    mine = sum(
        exchange(
            [lax.dynamic_slice_in_dim(piece, (c ^ k) * sub, sub) for k in range(parts)], "cols"
        )
    )
    mine = (mine * (1.0 / math.sqrt(total_nodes))).astype(BF16)
    whole = jnp.zeros((parts * sub, hidden), BF16)
    for k, part in enumerate(exchange([mine] * parts, "cols")):
        whole = lax.dynamic_update_slice_in_dim(whole, part, (c ^ k) * sub, 0)
    whole = across_rows(jnp.broadcast_to(whole[None], (partitions, *whole.shape)))
    whole = whole.reshape(2, parts * width, hidden).astype(F32)

    local, remote = pull(col, colref, grad_chunks, adj_vals, slots)
    returned = across_rows(remote.reshape(partitions, -1, width)).reshape(slots * tile, width)
    grad_feats = finish(col, wanted, self_parts, local, returned, tile)
    return (act, whole[0], whole[1], grad_feats)


def solution(mesh):
    in_specs = (
        P("rows", "cols"),
        P("rows", None, None, None),
        P("rows", None),
        P("rows", None, None),
        P(),
        P(),
        P(("rows", "cols"), None),
    )
    out_specs = (P(("rows", "cols"), None), P(), P(), P("rows", "cols"))
    return jax.shard_map(body, mesh=mesh, in_specs=in_specs, out_specs=out_specs, check_vma=False)
```

```python
import math

import jax
import jax.numpy as jnp
from jax import lax
from jax.experimental import pallas as pl
from jax.experimental.pallas import tpu as pltpu
from jax.sharding import PartitionSpec as P


BF16, F32 = jnp.bfloat16, jnp.float32
CHUNKS = 2
VMEM_LIMIT = 56 * 1024 * 1024


def params(dims):
    return pltpu.CompilerParams(
        dimension_semantics=("arbitrary",) * dims, vmem_limit_bytes=VMEM_LIMIT
    )


def full(shape):
    return pl.BlockSpec(shape, lambda *_: (0,) * len(shape))


def rows_at(index, tile):
    return pl.ds(pl.multiple_of(index * tile, tile), tile)


SMEM = pl.BlockSpec(memory_space=pltpu.SMEM)
ANY = pl.BlockSpec(memory_space=pl.ANY)


def id_rows(refs):
    rows = []
    for ref in refs:
        rows += [(ref, j) for j in range(ref.shape[0])]
    return rows


def select_tiles(row, ids, feats, tile, cap):
    count, width = sum(a.shape[0] for a in ids), feats.shape[1]

    def kernel(row_ref, *refs):
        id_refs, feats_ref = refs[: len(ids)], refs[len(ids)]
        outs, sems = refs[len(ids) + 1 : -1], refs[-1]
        where = id_rows(id_refs)
        copies = []
        for k in range(1, count):
            ref, j = where[k]
            for s in range(cap):
                source = jnp.maximum(ref[j, row_ref[0] * cap + s], 0)
                copies.append(
                    pltpu.make_async_copy(
                        feats_ref.at[rows_at(source, tile)],
                        outs[k - 1].at[s * tile : (s + 1) * tile],
                        sems.at[(k - 1) * cap + s],
                    )
                )
                copies[-1].start()
        for copy in copies:
            copy.wait()

    return pl.pallas_call(
        kernel,
        out_shape=[jax.ShapeDtypeStruct((cap * tile, width), feats.dtype)] * (count - 1),
        grid=(1,),
        in_specs=[SMEM] * (1 + len(ids)) + [ANY],
        out_specs=[full((cap * tile, width))] * (count - 1),
        scratch_shapes=[pltpu.SemaphoreType.DMA(((count - 1) * cap,))],
        name="select_tiles",
    )(row, *ids, feats)


def aggregate(col, colref, feats, arrived, adj, chunk, parts):
    blocks, per_block, tile, _ = adj.shape
    width = feats.shape[1]
    own = feats.shape[0]
    step = arrived[0].shape[0]
    count = len(arrived)
    per_part = blocks // parts
    per_chunk = per_part // CHUNKS
    chunk_rows = per_chunk * tile

    def tile_of(k, t, col_ref):
        return (k ^ col_ref[0]) * per_part + chunk * per_chunk + t

    def kernel(col_ref, colref_ref, feats_ref, *refs):
        arrived_refs, refs = refs[:count], refs[count:]
        adj_refs, outs, pool = refs[:parts], refs[parts : 2 * parts], refs[-1]
        t = pl.program_id(0)

        @pl.when(t == 0)
        def _():
            pool[:own, :] = feats_ref[...]
            for n, ref in enumerate(arrived_refs):
                pool[own + (n + 1) * step : own + (n + 2) * step, :] = ref[...]

        for k in range(parts):
            b = tile_of(k, t, col_ref)
            right = jnp.concatenate(
                [pool[rows_at(colref_ref[b, q], tile), :] for q in range(per_block)], axis=0
            )
            left = jnp.concatenate([adj_refs[k][0, q] for q in range(per_block)], axis=1)
            outs[k][...] = jnp.dot(left, right, preferred_element_type=F32).astype(BF16)

    def adj_spec(k):
        return pl.BlockSpec(
            (1, per_block, tile, tile), lambda t, c, r: (tile_of(k, t, c), 0, 0, 0)
        )

    return pl.pallas_call(
        kernel,
        out_shape=[jax.ShapeDtypeStruct((chunk_rows, width), BF16)] * parts,
        grid_spec=pltpu.PrefetchScalarGridSpec(
            num_scalar_prefetch=2,
            grid=(per_chunk,),
            in_specs=[full(feats.shape)]
            + [full(a.shape) for a in arrived]
            + [adj_spec(k) for k in range(parts)],
            out_specs=[pl.BlockSpec((tile, width), lambda t, c, r: (t, 0))] * parts,
            scratch_shapes=[pltpu.VMEM((own + (count + 1) * step, width), BF16)],
        ),
        compiler_params=params(1),
        name="aggregate",
    )(col, colref, feats, *arrived, *[adj] * parts)


def permuted(w_ref, col_ref, parts, width):
    return jnp.concatenate(
        [w_ref[rows_at(k ^ col_ref[0], width), :] for k in range(parts)], axis=0
    )


NT = (((1,), (1,)), ((), ()))
TN = (((0,), (0,)), ((), ()))


def dense(col, feat_rows, agg_parts, w_self, w_neigh, grad_out, act_prev, chunk):
    parts = len(agg_parts)
    chunk_rows, width = agg_parts[0].shape
    hidden = w_self.shape[1]
    steps = 2
    rows = chunk_rows // steps
    root = math.sqrt(2.0 / math.pi)

    def kernel(col_ref, *refs):
        f_ref, a_refs = refs[0], refs[1 : 1 + parts]
        ws_ref, wn_ref, go_ref = refs[1 + parts : 4 + parts]
        outs = refs[4 + parts + (act_prev is not None) :]
        act_ref, g_ref, back = outs[0], outs[1], outs[2:]
        ws = ws_ref[...]
        wn = permuted(wn_ref, col_ref, parts, width)
        f = jnp.concatenate([f_ref[j] for j in range(parts)], axis=1)
        a = jnp.concatenate([r[...] for r in a_refs], axis=1)
        v = jnp.dot(f, ws, preferred_element_type=F32) + jnp.dot(a, wn, preferred_element_type=F32)
        square = v * v
        tanh = jnp.tanh(root * (v + 0.044715 * (square * v)))
        half = 0.5 * (1.0 + tanh)
        act_ref[...] = (v * half).astype(BF16)
        slope = half + 0.5 * v * (1.0 - tanh * tanh) * (root * (1.0 + 3 * 0.044715 * square))
        g = (go_ref[...].astype(F32) * slope).astype(BF16)
        g_ref[...] = g
        spread = lax.dot_general(g, wn, NT, preferred_element_type=F32).astype(BF16)
        for k, out in enumerate(back):
            out[...] = spread[:, k * width : (k + 1) * width]

    offset = chunk * steps
    in_specs = (
        [pl.BlockSpec((parts, rows, width), lambda i, c: (0, offset + i, 0))]
        + [pl.BlockSpec((rows, width), lambda i, c: (i, 0))] * parts
        + [full(w_self.shape), full(w_neigh.shape)]
        + [pl.BlockSpec((rows, hidden), lambda i, c: (offset + i, 0))]
    )
    args = [col, feat_rows, *agg_parts, w_self, w_neigh, grad_out]
    aliases = {}
    if act_prev is not None:
        in_specs.append(pl.BlockSpec(memory_space=pl.ANY))
        aliases = {len(args): 0}
        args.append(act_prev)
    return pl.pallas_call(
        kernel,
        out_shape=[
            jax.ShapeDtypeStruct((chunk_rows * CHUNKS, hidden), BF16),
            jax.ShapeDtypeStruct((chunk_rows, hidden), BF16),
        ]
        + [jax.ShapeDtypeStruct((chunk_rows, width), BF16)] * parts,
        grid_spec=pltpu.PrefetchScalarGridSpec(
            num_scalar_prefetch=1,
            grid=(steps,),
            in_specs=in_specs,
            out_specs=[
                pl.BlockSpec((rows, hidden), lambda i, c: (offset + i, 0)),
                pl.BlockSpec((rows, hidden), lambda i, c: (i, 0)),
            ]
            + [pl.BlockSpec((rows, width), lambda i, c: (i, 0))] * parts,
        ),
        input_output_aliases=aliases,
        compiler_params=params(1),
        name="dense",
    )(*args)


def weights(col, row, feat_rows, agg_chunks, grads, w_self):
    parts, rows, width = feat_rows.shape
    hidden = w_self.shape[1]

    def kernel(col_ref, row_ref, *refs):
        f_ref, refs = refs[0], refs[1:]
        a_refs, refs = refs[: parts * CHUNKS], refs[parts * CHUNKS :]
        g_refs, ws_ref = refs[:CHUNKS], refs[CHUNKS]
        keep_ref, send_ref, *s_refs = refs[CHUNKS + 1 :]
        g = jnp.concatenate([r[...] for r in g_refs], axis=0)
        ws = permuted(ws_ref, col_ref, parts, width)
        s = lax.dot_general(g, ws, NT, preferred_element_type=F32).astype(BF16)
        for k, out in enumerate(s_refs):
            out[...] = s[:, k * width : (k + 1) * width]

        def emit(self_ref, neigh_ref):
            g = jnp.concatenate([r[...] for r in g_refs], axis=0)
            for k in range(parts):
                self_ref[k * width : (k + 1) * width, :] = lax.dot_general(
                    f_ref[k], g, TN, preferred_element_type=F32
                )
                a = jnp.concatenate([a_refs[h * parts + k][...] for h in range(CHUNKS)], axis=0)
                neigh_ref[rows_at(k ^ col_ref[0], width), :] = lax.dot_general(
                    a, g, TN, preferred_element_type=F32
                )

        even = row_ref[0] % 2 == 0
        pl.when(even)(lambda: emit(keep_ref, send_ref))
        pl.when(jnp.logical_not(even))(lambda: emit(send_ref, keep_ref))

    args = [feat_rows, *[a for chunk in agg_chunks for a in chunk], *grads, w_self]
    out_shape = [jax.ShapeDtypeStruct((parts * width, hidden), F32)] * 2 + [
        jax.ShapeDtypeStruct((rows, width), BF16)
    ] * parts
    return pl.pallas_call(
        kernel,
        out_shape=out_shape,
        grid_spec=pltpu.PrefetchScalarGridSpec(
            num_scalar_prefetch=2,
            grid=(1,),
            in_specs=[full(a.shape) for a in args],
            out_specs=[full(o.shape) for o in out_shape],
        ),
        compiler_params=params(1),
        name="weights",
    )(col, row, *args)


def combine(row, keep, received, chips):
    total, hidden = keep.shape
    rows = total // chips

    def kernel(row_ref, keep_ref, received_ref, *outs):
        for q, out in enumerate(outs):
            at = rows_at((row_ref[0] // 2) ^ q, rows)
            out[...] = keep_ref[at, :] + received_ref[at, :]

    return pl.pallas_call(
        kernel,
        out_shape=[jax.ShapeDtypeStruct((rows, hidden), F32)] * chips,
        grid_spec=pltpu.PrefetchScalarGridSpec(
            num_scalar_prefetch=1,
            grid=(1,),
            in_specs=[full(keep.shape)] * 2,
            out_specs=[full((rows, hidden))] * chips,
        ),
        compiler_params=params(1),
        name="combine",
    )(row, keep, received)


def assemble(row, pieces):
    rows, hidden = pieces[0].shape
    chips = len(pieces)

    def kernel(row_ref, *refs):
        for q in range(chips):
            refs[-1][rows_at((row_ref[0] // 2) ^ q, rows), :] = refs[q][...]

    return pl.pallas_call(
        kernel,
        out_shape=jax.ShapeDtypeStruct((chips * rows, hidden), BF16),
        grid_spec=pltpu.PrefetchScalarGridSpec(
            num_scalar_prefetch=1,
            grid=(1,),
            in_specs=[full((rows, hidden))] * chips,
            out_specs=full((chips * rows, hidden)),
        ),
        compiler_params=params(1),
        name="assemble",
    )(row, *pieces)


def widen(row, mine, other):
    def kernel(row_ref, mine_ref, other_ref, self_ref, neigh_ref):
        even = row_ref[0] % 2 == 0
        first, second = mine_ref[...].astype(F32), other_ref[...].astype(F32)
        self_ref[...] = jnp.where(even, first, second)
        neigh_ref[...] = jnp.where(even, second, first)

    return pl.pallas_call(
        kernel,
        out_shape=[jax.ShapeDtypeStruct(mine.shape, F32)] * 2,
        grid_spec=pltpu.PrefetchScalarGridSpec(
            num_scalar_prefetch=1,
            grid=(1,),
            in_specs=[full(mine.shape)] * 2,
            out_specs=[full(mine.shape)] * 2,
        ),
        compiler_params=params(1),
        name="widen",
    )(row, mine, other)


def pull(col, colref, grads, adj, partitions, cap, chunk, before):
    blocks, per_block, tile, _ = adj.shape
    parts = len(grads)
    _, width = grads[0].shape
    per_part = blocks // parts
    steps = per_part // CHUNKS
    last = chunk == CHUNKS - 1
    pool = blocks + partitions * cap
    extra = [] if before is None else [before]

    def kernel(col_ref, colref_ref, *refs):
        g_refs, adj_refs = refs[:parts], refs[parts : 2 * parts]
        refs = refs[2 * parts :]
        before_ref = refs[: len(extra)]
        outs, acc, sem = refs[len(extra) : -2], refs[-2], refs[-1]
        t = pl.program_id(0)

        @pl.when(t == 0)
        def _():
            if extra:
                copy = pltpu.make_async_copy(before_ref[0], acc, sem)
                copy.start()
                copy.wait()
            else:
                acc[...] = jnp.zeros_like(acc)

        for k in range(parts):
            b = (k ^ col_ref[0]) * per_part + chunk * steps + t
            turned = g_refs[k][rows_at(t, tile), :].T
            for q in range(0, per_block, 2):
                pair = jnp.concatenate([adj_refs[k][0, q], adj_refs[k][0, q + 1]], axis=1)
                both = jnp.dot(turned, pair, preferred_element_type=F32)
                acc[colref_ref[b, q]] += both[:, :tile]
                acc[colref_ref[b, q + 1]] += both[:, tile:]

        @pl.when(t == steps - 1)
        def _():
            if last:
                for n, out in enumerate(outs):
                    first = blocks + n * cap if n else 0
                    for s in range(out.shape[0] // tile):
                        out[s * tile : (s + 1) * tile, :] = acc[first + s].T.astype(BF16)
            else:
                copy = pltpu.make_async_copy(acc, outs[0], sem)
                copy.start()
                copy.wait()

    def adj_spec(k):
        return pl.BlockSpec(
            (1, per_block, tile, tile),
            lambda t, c, r: ((k ^ c[0]) * per_part + chunk * steps + t, 0, 0, 0),
        )

    if last:
        out_shape = [jax.ShapeDtypeStruct((blocks * tile, width), BF16)]
        out_shape += [jax.ShapeDtypeStruct((cap * tile, width), BF16)] * (partitions - 1)
        out_specs = [full(o.shape) for o in out_shape]
    else:
        out_shape = [jax.ShapeDtypeStruct((pool, width, tile), F32)]
        out_specs = [ANY]
    return pl.pallas_call(
        kernel,
        out_shape=out_shape,
        grid_spec=pltpu.PrefetchScalarGridSpec(
            num_scalar_prefetch=2,
            grid=(steps,),
            in_specs=[full(g.shape) for g in grads]
            + [adj_spec(k) for k in range(parts)]
            + [ANY] * len(extra),
            out_specs=out_specs,
            scratch_shapes=[
                pltpu.VMEM((pool, width, tile), F32),
                pltpu.SemaphoreType.DMA(()),
            ],
        ),
        compiler_params=params(1),
        name="pull",
    )(col, colref, *grads, *[adj] * parts, *extra)


def finish(col, row, ids, self_parts, local, returned, tile, cap):
    parts = len(self_parts)
    rows, _ = self_parts[0].shape
    count = len(returned)

    def kernel(col_ref, row_ref, *refs):
        id_refs, refs = refs[: len(ids)], refs[len(ids) :]
        s_refs, local_ref = refs[:parts], refs[parts]
        returned_refs, out_ref = refs[parts + 1 : -1], refs[-1]
        where = id_rows(id_refs)
        for k in range(parts):
            at = rows_at(k ^ col_ref[0], rows)
            out_ref[at, :] = s_refs[k][...].astype(F32) + local_ref[at, :].astype(F32)
        for n in range(count):
            ref, j = where[n + 1]
            for s in range(cap):
                target = ref[j, row_ref[0] * cap + s]

                @pl.when(target >= 0)
                def _():
                    out_ref[rows_at(target, tile), :] += returned_refs[n][
                        s * tile : (s + 1) * tile, :
                    ].astype(F32)

    args = [*self_parts, local, *returned]
    return pl.pallas_call(
        kernel,
        out_shape=jax.ShapeDtypeStruct(local.shape, F32),
        grid_spec=pltpu.PrefetchScalarGridSpec(
            num_scalar_prefetch=2,
            grid=(1,),
            in_specs=[SMEM] * len(ids) + [full(a.shape) for a in args],
            out_specs=full(local.shape),
        ),
        compiler_params=params(1),
        name="finish",
    )(col, row, *ids, *args)


def swap(x, axis, k):
    n = lax.axis_size(axis)
    return lax.ppermute(x, axis, [(i, i ^ k) for i in range(n)])


def exchange(pieces, axis, stride=1):
    out = [pieces[0]]
    for k in range(1, len(pieces)):
        out.append(swap(pieces[k], axis, k * stride))
    return out


def tree_sum(parts):
    while len(parts) > 1:
        parts = [parts[n] + parts[n + 1] for n in range(0, len(parts), 2)]
    return parts[0]


def body(feats, adj_vals, colref, fetch_ids, w_self, w_neigh, grad_out):
    node_rows, width = feats.shape
    blocks, _, tile, _ = adj_vals.shape
    partitions = lax.axis_size("rows")
    parts = lax.axis_size("cols")
    cap = fetch_ids.shape[2]
    chips = partitions // 2
    total_nodes = node_rows * partitions
    row_index, col_index = lax.axis_index("rows"), lax.axis_index("cols")
    col = col_index.astype(jnp.int32).reshape(1)
    row = row_index.astype(jnp.int32).reshape(1)

    feat_rows = lax.all_to_all(
        feats.reshape(parts, node_rows // parts, width), "cols", 0, 0, tiled=True
    )
    known = fetch_ids.reshape(1, partitions * cap)
    known = jnp.pad(known, ((0, 0), (0, -known.shape[1] % 128)))
    ids, hop = [known], 1
    while hop < partitions:
        ids.append(swap(known, "rows", hop))
        known = jnp.concatenate([known, ids[-1]], axis=0)
        hop *= 2
    outgoing = select_tiles(row, ids, feats, tile, cap)
    arrived = exchange([None, *outgoing], "rows")[1:]
    slot = jnp.maximum(colref - blocks, 0)
    slot = ((slot // cap) ^ row_index) * cap + slot % cap
    places = jnp.where(colref < blocks, colref, blocks + slot).astype(jnp.int32)

    agg_chunks = []
    for h in range(CHUNKS):
        pieces = aggregate(col, places, feats, arrived, adj_vals, h, parts)
        agg_chunks.append(exchange(pieces, "cols"))
    act, grads, grad_chunks = None, [], []
    for h in range(CHUNKS):
        act, g, *back = dense(
            col, feat_rows, agg_chunks[h], w_self, w_neigh, grad_out, act, h
        )
        grads.append(g)
        grad_chunks.append(exchange(back, "cols"))
    keep, send, *self_rows = weights(col, row, feat_rows, agg_chunks, grads, w_self)
    self_parts = exchange(self_rows, "cols")

    received = exchange([keep, send], "rows")[1]
    pieces = combine(row, keep, received, chips)
    partial = tree_sum(exchange(pieces, "rows", 2)).astype(BF16)
    mine = tree_sum([p.astype(F32) for p in exchange([partial] * parts, "cols")])
    mine = (mine * (1.0 / math.sqrt(total_nodes))).astype(BF16)
    half = assemble(row, exchange([mine] * chips, "rows", 2))
    grad_self_w, grad_neigh_w = widen(row, half, exchange([half, half], "rows")[1])

    before = None
    for h in range(CHUNKS):
        before, *remote = pull(col, places, grad_chunks[h], adj_vals, partitions, cap, h, before)
    returned = exchange([None, *remote], "rows")[1:]
    grad_feats = finish(col, row, ids, self_parts, before, returned, tile, cap)
    return (act, grad_self_w, grad_neigh_w, grad_feats)


def solution(mesh):
    in_specs = (
        P("rows", "cols"),
        P("rows", None, None, None),
        P("rows", None),
        P("rows", None, None),
        P(),
        P(),
        P(("rows", "cols"), None),
    )
    out_specs = (P(("rows", "cols"), None), P(), P(), P("rows", "cols"))
    return jax.shard_map(body, mesh=mesh, in_specs=in_specs, out_specs=out_specs, check_vma=False)
```

```python
import math

import jax
import jax.numpy as jnp
from jax import lax
from jax.experimental import pallas as pl
from jax.experimental.pallas import tpu as pltpu
from jax.sharding import PartitionSpec as P


BF16, F32 = jnp.bfloat16, jnp.float32
CHUNKS = 2
VMEM_LIMIT = 24 * 1024 * 1024


def params():
    return pltpu.CompilerParams(dimension_semantics=("arbitrary",), vmem_limit_bytes=VMEM_LIMIT)


def full(shape):
    return pl.BlockSpec(shape, lambda *_: (0,) * len(shape))


def rows_at(index, tile):
    return pl.ds(pl.multiple_of(index * tile, tile), tile)


SMEM = pl.BlockSpec(memory_space=pltpu.SMEM)
ANY = pl.BlockSpec(memory_space=pl.ANY)


def id_rows(refs):
    rows = []
    for ref in refs:
        rows += [(ref, j) for j in range(ref.shape[0])]
    return rows


def begin(sources, targets, sems):
    copies = [
        pltpu.make_async_copy(source, target, sems.at[n])
        for n, (source, target) in enumerate(zip(sources, targets))
    ]
    for copy in copies:
        copy.start()
    return copies


def load(sources, targets, sems):
    for copy in begin(sources, targets, sems):
        copy.wait()


def select_tiles(row, ids, feats, tile, cap):
    count, width = sum(a.shape[0] for a in ids), feats.shape[1]

    def kernel(row_ref, *refs):
        id_refs, feats_ref = refs[: len(ids)], refs[len(ids)]
        outs, sems = refs[len(ids) + 1 : -1], refs[-1]
        where = id_rows(id_refs)
        copies = []
        for k in range(1, count):
            ref, j = where[k]
            for s in range(cap):
                source = jnp.maximum(ref[j, row_ref[0] * cap + s], 0)
                copies.append(
                    pltpu.make_async_copy(
                        feats_ref.at[rows_at(source, tile)],
                        outs[k - 1].at[s * tile : (s + 1) * tile],
                        sems.at[(k - 1) * cap + s],
                    )
                )
                copies[-1].start()
        for copy in copies:
            copy.wait()

    return pl.pallas_call(
        kernel,
        out_shape=[jax.ShapeDtypeStruct((cap * tile, width), feats.dtype)] * (count - 1),
        grid=(1,),
        in_specs=[SMEM] * (1 + len(ids)) + [ANY],
        out_specs=[full((cap * tile, width))] * (count - 1),
        scratch_shapes=[pltpu.SemaphoreType.DMA(((count - 1) * cap,))],
        compiler_params=params(),
        name="select_tiles",
    )(row, *ids, feats)


def aggregate(col, colref, sources, adj, chunk, parts, pool_rows):
    blocks, per_block, tile, _ = adj.shape
    width = sources[0].shape[1]
    count = len(sources)
    fresh = count > 1
    per_part = blocks // parts
    per_chunk = per_part // CHUNKS
    chunk_rows = per_chunk * tile
    shapes = [(chunk_rows, width)] * parts + [(pool_rows, width)] * fresh

    def kernel(col_ref, colref_ref, *refs):
        source_refs, adj_ref, outs = refs[:count], refs[count], refs[count + 1 : -3]
        held, sems, adj_sems = refs[-3:]
        pool = outs[parts] if fresh else source_refs[0]

        def first(k):
            return (k ^ col_ref[0]) * per_part + chunk * per_chunk

        def fetch(t, k):
            return pltpu.make_async_copy(
                adj_ref.at[first(k) + t], held.at[t, k], adj_sems.at[t, k]
            )

        copies = []
        if fresh:
            own, step = source_refs[0].shape[0], source_refs[1].shape[0]
            targets = [pool.at[:own]]
            for n in range(1, count):
                targets.append(pool.at[own + n * step : own + (n + 1) * step])
            copies = begin(source_refs, targets, sems)
        for t in range(per_chunk):
            for k in range(parts):
                fetch(t, k).start()
        for copy in copies:
            copy.wait()

        @pl.loop(0, per_chunk)
        def _(t):
            for k in range(parts):
                fetch(t, k).wait()
            for k in range(parts):
                b = first(k) + t
                right = jnp.concatenate(
                    [pool[rows_at(colref_ref[q, b], tile), :] for q in range(per_block)], axis=0
                )
                left = jnp.concatenate([held[t, k, q] for q in range(per_block)], axis=1)
                result = jnp.dot(left, right, preferred_element_type=F32)
                outs[k][rows_at(t, tile), :] = result.astype(BF16)

    return pl.pallas_call(
        kernel,
        out_shape=[jax.ShapeDtypeStruct(shape, BF16) for shape in shapes],
        grid_spec=pltpu.PrefetchScalarGridSpec(
            num_scalar_prefetch=2,
            grid=(1,),
            in_specs=([ANY] * count if fresh else [full(sources[0].shape)]) + [ANY],
            out_specs=[full(shape) for shape in shapes],
            scratch_shapes=[
                pltpu.VMEM((per_chunk, parts, per_block, tile, tile), BF16),
                pltpu.SemaphoreType.DMA((count,)),
                pltpu.SemaphoreType.DMA((per_chunk, parts)),
            ],
        ),
        compiler_params=params(),
        name="aggregate",
    )(col, colref, *sources, adj)


def permuted(w_ref, col_ref, parts, width):
    return jnp.concatenate(
        [w_ref[rows_at(k ^ col_ref[0], width), :] for k in range(parts)], axis=0
    )


NT = (((1,), (1,)), ((), ()))
TN = (((0,), (0,)), ((), ()))


def dense(col, feat_rows, agg_parts, w_self, w_neigh, grad_out, act_prev, chunk):
    parts = len(agg_parts)
    chunk_rows, width = agg_parts[0].shape
    hidden = w_self.shape[1]
    steps = 2
    rows = chunk_rows // steps
    root = math.sqrt(2.0 / math.pi)

    def kernel(col_ref, *refs):
        f_ref, a_refs = refs[0], refs[1 : 1 + parts]
        ws_ref, wn_ref, go_ref = refs[1 + parts : 4 + parts]
        outs = refs[4 + parts + (act_prev is not None) :]
        act_ref, g_ref, back = outs[0], outs[1], outs[2:]
        ws = ws_ref[...]
        wn = permuted(wn_ref, col_ref, parts, width)
        f = jnp.concatenate([f_ref[j] for j in range(parts)], axis=1)
        a = jnp.concatenate([r[...] for r in a_refs], axis=1)
        v = jnp.dot(f, ws, preferred_element_type=F32) + jnp.dot(a, wn, preferred_element_type=F32)
        square = v * v
        tanh = jnp.tanh(root * (v + 0.044715 * (square * v)))
        half = 0.5 * (1.0 + tanh)
        act_ref[...] = (v * half).astype(BF16)
        slope = half + 0.5 * v * (1.0 - tanh * tanh) * (root * (1.0 + 3 * 0.044715 * square))
        g = (go_ref[...].astype(F32) * slope).astype(BF16)
        g_ref[...] = g
        spread = lax.dot_general(g, wn, NT, preferred_element_type=F32).astype(BF16)
        for k, out in enumerate(back):
            out[...] = spread[:, k * width : (k + 1) * width]

    offset = chunk * steps
    in_specs = (
        [pl.BlockSpec((parts, rows, width), lambda i, c: (0, offset + i, 0))]
        + [pl.BlockSpec((rows, width), lambda i, c: (i, 0))] * parts
        + [full(w_self.shape), full(w_neigh.shape)]
        + [pl.BlockSpec((rows, hidden), lambda i, c: (offset + i, 0))]
    )
    args = [col, feat_rows, *agg_parts, w_self, w_neigh, grad_out]
    aliases = {}
    if act_prev is not None:
        in_specs.append(pl.BlockSpec(memory_space=pl.ANY))
        aliases = {len(args): 0}
        args.append(act_prev)
    return pl.pallas_call(
        kernel,
        out_shape=[
            jax.ShapeDtypeStruct((chunk_rows * CHUNKS, hidden), BF16),
            jax.ShapeDtypeStruct((chunk_rows, hidden), BF16),
        ]
        + [jax.ShapeDtypeStruct((chunk_rows, width), BF16)] * parts,
        grid_spec=pltpu.PrefetchScalarGridSpec(
            num_scalar_prefetch=1,
            grid=(steps,),
            in_specs=in_specs,
            out_specs=[
                pl.BlockSpec((rows, hidden), lambda i, c: (offset + i, 0)),
                pl.BlockSpec((rows, hidden), lambda i, c: (i, 0)),
            ]
            + [pl.BlockSpec((rows, width), lambda i, c: (i, 0))] * parts,
        ),
        input_output_aliases=aliases,
        compiler_params=params(),
        name="dense",
    )(*args)


def weights(col, row, feat_rows, agg_chunks, grads, w_self):
    parts, rows, width = feat_rows.shape
    hidden = w_self.shape[1]

    def kernel(col_ref, row_ref, *refs):
        f_ref, refs = refs[0], refs[1:]
        a_refs, refs = refs[: parts * CHUNKS], refs[parts * CHUNKS :]
        g_refs, ws_ref = refs[:CHUNKS], refs[CHUNKS]
        keep_ref, send_ref, *s_refs = refs[CHUNKS + 1 :]
        g = jnp.concatenate([r[...] for r in g_refs], axis=0)
        ws = permuted(ws_ref, col_ref, parts, width)
        s = lax.dot_general(g, ws, NT, preferred_element_type=F32).astype(BF16)
        for k, out in enumerate(s_refs):
            out[...] = s[:, k * width : (k + 1) * width]

        def emit(self_ref, neigh_ref):
            g = jnp.concatenate([r[...] for r in g_refs], axis=0)
            for k in range(parts):
                self_ref[k * width : (k + 1) * width, :] = lax.dot_general(
                    f_ref[k], g, TN, preferred_element_type=F32
                )
                a = jnp.concatenate([a_refs[h * parts + k][...] for h in range(CHUNKS)], axis=0)
                neigh_ref[rows_at(k ^ col_ref[0], width), :] = lax.dot_general(
                    a, g, TN, preferred_element_type=F32
                )

        even = row_ref[0] % 2 == 0
        pl.when(even)(lambda: emit(keep_ref, send_ref))
        pl.when(jnp.logical_not(even))(lambda: emit(send_ref, keep_ref))

    args = [feat_rows, *[a for chunk in agg_chunks for a in chunk], *grads, w_self]
    out_shape = [jax.ShapeDtypeStruct((parts * width, hidden), F32)] * 2 + [
        jax.ShapeDtypeStruct((rows, width), BF16)
    ] * parts
    return pl.pallas_call(
        kernel,
        out_shape=out_shape,
        grid_spec=pltpu.PrefetchScalarGridSpec(
            num_scalar_prefetch=2,
            grid=(1,),
            in_specs=[full(a.shape) for a in args],
            out_specs=[full(o.shape) for o in out_shape],
        ),
        compiler_params=params(),
        name="weights",
    )(col, row, *args)


def combine(row, keep, received, chips):
    total, hidden = keep.shape
    rows = total // chips

    def kernel(row_ref, keep_ref, received_ref, *outs):
        for q, out in enumerate(outs):
            at = rows_at((row_ref[0] // 2) ^ q, rows)
            out[...] = keep_ref[at, :] + received_ref[at, :]

    return pl.pallas_call(
        kernel,
        out_shape=[jax.ShapeDtypeStruct((rows, hidden), F32)] * chips,
        grid_spec=pltpu.PrefetchScalarGridSpec(
            num_scalar_prefetch=1,
            grid=(1,),
            in_specs=[full(keep.shape)] * 2,
            out_specs=[full((rows, hidden))] * chips,
        ),
        compiler_params=params(),
        name="combine",
    )(row, keep, received)


def widen(row, mine, other):
    rows, hidden = mine[0].shape
    chips = len(mine)

    def kernel(row_ref, *refs):
        sources, outs = refs[: 2 * chips], refs[2 * chips : 2 * chips + 2]
        pieces, wide, sems, out_sems = refs[2 * chips + 2 :]
        copies = begin(sources, [pieces.at[n] for n in range(2 * chips)], sems)
        even = row_ref[0] % 2 == 0
        writes = []
        for q in range(chips):
            at = rows_at((row_ref[0] // 2) ^ q, rows)
            copies[q].wait()
            copies[chips + q].wait()
            first, second = pieces[q].astype(F32), pieces[chips + q].astype(F32)
            wide[0, q] = jnp.where(even, first, second)
            wide[1, q] = jnp.where(even, second, first)
            for n, out in enumerate(outs):
                writes.append(
                    pltpu.make_async_copy(wide.at[n, q], out.at[at], out_sems.at[n, q])
                )
                writes[-1].start()
        for write in writes:
            write.wait()

    return pl.pallas_call(
        kernel,
        out_shape=[jax.ShapeDtypeStruct((chips * rows, hidden), F32)] * 2,
        grid_spec=pltpu.PrefetchScalarGridSpec(
            num_scalar_prefetch=1,
            grid=(1,),
            in_specs=[ANY] * (2 * chips),
            out_specs=[ANY] * 2,
            scratch_shapes=[
                pltpu.VMEM((2 * chips, rows, hidden), BF16),
                pltpu.VMEM((2, chips, rows, hidden), F32),
                pltpu.SemaphoreType.DMA((2 * chips,)),
                pltpu.SemaphoreType.DMA((2, chips)),
            ],
        ),
        compiler_params=params(),
        name="widen",
    )(row, *mine, *other)


def pull(col, row, colref, grads, adj, partitions, cap, chunk, before):
    blocks, per_block, tile, _ = adj.shape
    parts = len(grads)
    chunk_rows, width = grads[0].shape
    per_part = blocks // parts
    steps = per_part // CHUNKS
    last = chunk == CHUNKS - 1
    pool = blocks + partitions * cap
    extra = [] if before is None else [before]

    def kernel(col_ref, row_ref, colref_ref, *refs):
        g_refs, adj_ref, refs = refs[:parts], refs[parts], refs[parts + 1 :]
        before_ref, outs = refs[: len(extra)], refs[len(extra) : -5]
        grad, acc, held, sems, adj_sems = refs[-5:]

        def first(k):
            return (k ^ col_ref[0]) * per_part + chunk * steps

        def fetch(t, k):
            return pltpu.make_async_copy(
                adj_ref.at[first(k) + t], held.at[t, k], adj_sems.at[t, k]
            )

        sources, targets = list(g_refs), [grad.at[k] for k in range(parts)]
        if extra:
            sources.append(before_ref[0])
            targets.append(acc)
        copies = begin(sources, targets, sems)
        for t in range(steps):
            for k in range(parts):
                fetch(t, k).start()
        if not extra:
            acc[...] = jnp.zeros_like(acc)
        for copy in copies:
            copy.wait()

        @pl.loop(0, steps)
        def _(t):
            for k in range(parts):
                fetch(t, k).wait()
            for k in range(parts):
                b = first(k) + t
                turned = grad[k, rows_at(t, tile), :].T
                for q in range(0, per_block, 2):
                    pair = jnp.concatenate([held[t, k, q], held[t, k, q + 1]], axis=1)
                    both = jnp.dot(turned, pair, preferred_element_type=F32)
                    acc[colref_ref[q, b]] += both[:, :tile]
                    acc[colref_ref[q + 1, b]] += both[:, tile:]

        if last:
            local_ref, remote_ref = outs
            for s in range(blocks):
                local_ref[s * tile : (s + 1) * tile, :] = acc[s].T.astype(BF16)
            for k in range(partitions):
                for s in range(cap):
                    remote_ref[k ^ row_ref[0], s * tile : (s + 1) * tile, :] = (
                        acc[blocks + k * cap + s].T.astype(BF16)
                    )
        else:
            load([acc], [outs[0]], sems)

    if last:
        out_shape = [jax.ShapeDtypeStruct((blocks * tile, width), BF16)]
        out_shape += [jax.ShapeDtypeStruct((partitions, cap * tile, width), BF16)]
        out_specs = [full(o.shape) for o in out_shape]
    else:
        out_shape = [jax.ShapeDtypeStruct((pool, width, tile), F32)]
        out_specs = [ANY]
    return pl.pallas_call(
        kernel,
        out_shape=out_shape,
        grid_spec=pltpu.PrefetchScalarGridSpec(
            num_scalar_prefetch=3,
            grid=(1,),
            in_specs=[ANY] * parts + [ANY] + [ANY] * len(extra),
            out_specs=out_specs,
            scratch_shapes=[
                pltpu.VMEM((parts, chunk_rows, width), BF16),
                pltpu.VMEM((pool, width, tile), F32),
                pltpu.VMEM((steps, parts, per_block, tile, tile), BF16),
                pltpu.SemaphoreType.DMA((parts + 1,)),
                pltpu.SemaphoreType.DMA((steps, parts)),
            ],
        ),
        compiler_params=params(),
        name="pull",
    )(col, row, colref, *grads, adj, *extra)


def finish(col, row, ids, self_parts, local, returned, tile, cap):
    parts = len(self_parts)
    rows, width = self_parts[0].shape
    count = returned.shape[0]

    def kernel(col_ref, row_ref, *refs):
        id_refs, refs = refs[: len(ids)], refs[len(ids) :]
        s_refs, (local_ref, returned_ref, out_ref, own, back, sems) = refs[:parts], refs[parts:]
        load([*s_refs, returned_ref], [*[own.at[k] for k in range(parts)], back], sems)
        where = id_rows(id_refs)
        for k in range(parts):
            at = rows_at(k ^ col_ref[0], rows)
            out_ref[at, :] = own[k].astype(F32) + local_ref[at, :].astype(F32)
        for n in range(1, count):
            ref, j = where[n]
            for s in range(cap):
                target = ref[j, row_ref[0] * cap + s]

                @pl.when(target >= 0)
                def _():
                    out_ref[rows_at(target, tile), :] += back[
                        n ^ row_ref[0], s * tile : (s + 1) * tile, :
                    ].astype(F32)

    return pl.pallas_call(
        kernel,
        out_shape=jax.ShapeDtypeStruct(local.shape, F32),
        grid_spec=pltpu.PrefetchScalarGridSpec(
            num_scalar_prefetch=2,
            grid=(1,),
            in_specs=[SMEM] * len(ids) + [ANY] * parts + [full(local.shape), ANY],
            out_specs=full(local.shape),
            scratch_shapes=[
                pltpu.VMEM((parts, rows, width), BF16),
                pltpu.VMEM(returned.shape, BF16),
                pltpu.SemaphoreType.DMA((parts + 1,)),
            ],
        ),
        compiler_params=params(),
        name="finish",
    )(col, row, *ids, *self_parts, local, returned)


def swap(x, axis, k):
    n = lax.axis_size(axis)
    return lax.ppermute(x, axis, [(i, i ^ k) for i in range(n)])


def exchange(pieces, axis, stride=1):
    out = [pieces[0]]
    for k in range(1, len(pieces)):
        out.append(swap(pieces[k], axis, k * stride))
    return out


def tree_sum(parts):
    while len(parts) > 1:
        parts = [parts[n] + parts[n + 1] for n in range(0, len(parts), 2)]
    return parts[0]


def body(feats, adj_vals, colref, fetch_ids, w_self, w_neigh, grad_out):
    node_rows, width = feats.shape
    blocks, _, tile, _ = adj_vals.shape
    partitions = lax.axis_size("rows")
    parts = lax.axis_size("cols")
    cap = fetch_ids.shape[2]
    chips = partitions // 2
    total_nodes = node_rows * partitions
    row_index, col_index = lax.axis_index("rows"), lax.axis_index("cols")
    col = col_index.astype(jnp.int32).reshape(1)
    row = row_index.astype(jnp.int32).reshape(1)

    feat_rows = lax.all_to_all(
        feats.reshape(parts, node_rows // parts, width), "cols", 0, 0, tiled=True
    )
    known = fetch_ids.reshape(1, partitions * cap)
    known = jnp.pad(known, ((0, 0), (0, -known.shape[1] % 128)))
    ids, hop = [known], 1
    while hop < partitions:
        ids.append(swap(known, "rows", hop))
        known = jnp.concatenate([known, ids[-1]], axis=0)
        hop *= 2
    outgoing = select_tiles(
        row, ids, pltpu.with_memory_space_constraint(feats, pltpu.HBM), tile, cap
    )
    arrived = exchange([None, *outgoing], "rows")[1:]
    pooled = colref.T
    slot = jnp.maximum(pooled - blocks, 0)
    slot = ((slot // cap) ^ row_index) * cap + slot % cap
    places = jnp.where(pooled < blocks, pooled, blocks + slot).astype(jnp.int32)

    adj_vals = pltpu.with_memory_space_constraint(adj_vals, pltpu.HBM)
    agg_chunks, sources = [], [feats, *arrived]
    pool_rows = (blocks + partitions * cap) * tile
    for h in range(CHUNKS):
        pieces = aggregate(col, places, sources, adj_vals, h, parts, pool_rows)
        sources = pieces[parts:] or sources
        agg_chunks.append(exchange(pieces[:parts], "cols"))
    act, grads, grad_chunks = None, [], []
    for h in range(CHUNKS):
        act, g, *back = dense(
            col, feat_rows, agg_chunks[h], w_self, w_neigh, grad_out, act, h
        )
        grads.append(g)
        grad_chunks.append(exchange(back, "cols"))
    keep, send, *self_rows = weights(col, row, feat_rows, agg_chunks, grads, w_self)
    self_parts = exchange(self_rows, "cols")

    received = exchange([keep, send], "rows")[1]
    pieces = combine(row, keep, received, chips)
    partial = tree_sum(exchange(pieces, "rows", 2)).astype(BF16)
    mine = tree_sum([p.astype(F32) for p in exchange([partial] * parts, "cols")])
    mine = (mine * (1.0 / math.sqrt(total_nodes))).astype(BF16)
    pieces = exchange([mine] * chips, "rows", 2)
    other = []
    for piece in pieces:
        other.append(swap(piece, "rows", 1))
    grad_self_w, grad_neigh_w = widen(row, pieces, other)

    before = None
    for h in range(CHUNKS):
        before, *remote = pull(
            col, row, places, grad_chunks[h], adj_vals, partitions, cap, h, before
        )
    returned = lax.all_to_all(remote[0], "rows", 0, 0, tiled=True)
    grad_feats = finish(col, row, ids, self_parts, before, returned, tile, cap)
    return (act, grad_self_w, grad_neigh_w, grad_feats)


def solution(mesh):
    in_specs = (
        P("rows", "cols"),
        P("rows", None, None, None),
        P("rows", None),
        P("rows", None, None),
        P(),
        P(),
        P(("rows", "cols"), None),
    )
    out_specs = (P(("rows", "cols"), None), P(), P(), P("rows", "cols"))
    return jax.shard_map(body, mesh=mesh, in_specs=in_specs, out_specs=out_specs, check_vma=False)
```

```python
import math

import jax
import jax.numpy as jnp
from jax import lax
from jax.experimental import pallas as pl
from jax.experimental.pallas import tpu as pltpu
from jax.sharding import PartitionSpec as P


BF16, F32 = jnp.bfloat16, jnp.float32
CHUNKS = 2
VMEM_LIMIT = 24 * 1024 * 1024


def params():
    return pltpu.CompilerParams(dimension_semantics=("arbitrary",), vmem_limit_bytes=VMEM_LIMIT)


def full(shape):
    return pl.BlockSpec(shape, lambda *_: (0,) * len(shape))


def rows_at(index, tile):
    return pl.ds(pl.multiple_of(index * tile, tile), tile)


SMEM = pl.BlockSpec(memory_space=pltpu.SMEM)
ANY = pl.BlockSpec(memory_space=pl.ANY)


def id_rows(refs):
    rows = []
    for ref in refs:
        rows += [(ref, j) for j in range(ref.shape[0])]
    return rows


def begin(sources, targets, sems):
    copies = [
        pltpu.make_async_copy(source, target, sems.at[n])
        for n, (source, target) in enumerate(zip(sources, targets))
    ]
    for copy in copies:
        copy.start()
    return copies


def load(sources, targets, sems):
    for copy in begin(sources, targets, sems):
        copy.wait()


def select_tiles(row, ids, feats, tile, cap):
    count, width = sum(a.shape[0] for a in ids), feats.shape[1]

    def kernel(row_ref, *refs):
        id_refs, feats_ref = refs[: len(ids)], refs[len(ids)]
        outs, sems = refs[len(ids) + 1 : -1], refs[-1]
        where = id_rows(id_refs)
        copies = []
        for k in range(1, count):
            ref, j = where[k]
            for s in range(cap):
                source = jnp.maximum(ref[j, row_ref[0] * cap + s], 0)
                copies.append(
                    pltpu.make_async_copy(
                        feats_ref.at[rows_at(source, tile)],
                        outs[k - 1].at[s * tile : (s + 1) * tile],
                        sems.at[(k - 1) * cap + s],
                    )
                )
                copies[-1].start()
        for copy in copies:
            copy.wait()

    return pl.pallas_call(
        kernel,
        out_shape=[jax.ShapeDtypeStruct((cap * tile, width), feats.dtype)] * (count - 1),
        grid=(1,),
        in_specs=[SMEM] * (1 + len(ids)) + [ANY],
        out_specs=[full((cap * tile, width))] * (count - 1),
        scratch_shapes=[pltpu.SemaphoreType.DMA(((count - 1) * cap,))],
        compiler_params=params(),
        name="select_tiles",
    )(row, *ids, feats)


def aggregate(col, colref, sources, adj, chunk, parts, pool_rows):
    blocks, per_block, tile, _ = adj.shape
    width = sources[0].shape[1]
    count = len(sources)
    fresh = count > 1
    per_part = blocks // parts
    per_chunk = per_part // CHUNKS
    chunk_rows = per_chunk * tile
    shapes = [(chunk_rows, width)] * parts + [(pool_rows, width)] * fresh

    def kernel(col_ref, colref_ref, *refs):
        source_refs, adj_ref, outs = refs[:count], refs[count], refs[count + 1 :]
        held, sems, adj_sems = refs[-3 - fresh : len(refs) - fresh]
        pool = refs[-1] if fresh else source_refs[0]

        def first(k):
            return (k ^ col_ref[0]) * per_part + chunk * per_chunk

        def fetch(t, k):
            return pltpu.make_async_copy(
                adj_ref.at[first(k) + t], held.at[t, k], adj_sems.at[t, k]
            )

        copies = []
        if fresh:
            own, step = source_refs[0].shape[0], source_refs[1].shape[0]
            targets = [pool.at[:own]]
            for n in range(1, count):
                targets.append(pool.at[own + n * step : own + (n + 1) * step])
            copies = begin(source_refs, targets, sems)
        for t in range(per_chunk):
            for k in range(parts):
                fetch(t, k).start()
        for copy in copies:
            copy.wait()
        passed = begin([pool], [outs[parts]], sems) if fresh else []

        @pl.loop(0, per_chunk)
        def _(t):
            for k in range(parts):
                fetch(t, k).wait()
            for k in range(parts):
                b = first(k) + t
                right = jnp.concatenate(
                    [pool[rows_at(colref_ref[q, b], tile), :] for q in range(per_block)], axis=0
                )
                left = jnp.concatenate([held[t, k, q] for q in range(per_block)], axis=1)
                result = jnp.dot(left, right, preferred_element_type=F32)
                outs[k][rows_at(t, tile), :] = result.astype(BF16)

        for copy in passed:
            copy.wait()

    return pl.pallas_call(
        kernel,
        out_shape=[jax.ShapeDtypeStruct(shape, BF16) for shape in shapes],
        grid_spec=pltpu.PrefetchScalarGridSpec(
            num_scalar_prefetch=2,
            grid=(1,),
            in_specs=([ANY] * count if fresh else [full(sources[0].shape)]) + [ANY],
            out_specs=[full((chunk_rows, width))] * parts + [ANY] * fresh,
            scratch_shapes=[
                pltpu.VMEM((per_chunk, parts, per_block, tile, tile), BF16),
                pltpu.SemaphoreType.DMA((count,)),
                pltpu.SemaphoreType.DMA((per_chunk, parts)),
            ]
            + [pltpu.VMEM((pool_rows, width), BF16)] * fresh,
        ),
        compiler_params=params(),
        name="aggregate",
    )(col, colref, *sources, adj)


def permuted(w_ref, col_ref, parts, width):
    return jnp.concatenate(
        [w_ref[rows_at(k ^ col_ref[0], width), :] for k in range(parts)], axis=0
    )


NT = (((1,), (1,)), ((), ()))
TN = (((0,), (0,)), ((), ()))


def dense(col, feat_rows, agg_parts, w_self, w_neigh, grad_out, act_prev, chunk):
    parts = len(agg_parts)
    chunk_rows, width = agg_parts[0].shape
    hidden = w_self.shape[1]
    steps = 2
    rows = chunk_rows // steps
    root = math.sqrt(2.0 / math.pi)

    def kernel(col_ref, *refs):
        f_ref, a_refs = refs[0], refs[1 : 1 + parts]
        ws_ref, wn_ref, go_ref = refs[1 + parts : 4 + parts]
        outs = refs[4 + parts + (act_prev is not None) :]
        act_ref, g_ref, back = outs[0], outs[1], outs[2:]
        ws = ws_ref[...]
        wn = permuted(wn_ref, col_ref, parts, width)
        f = jnp.concatenate([f_ref[j] for j in range(parts)], axis=1)
        a = jnp.concatenate([r[...] for r in a_refs], axis=1)
        v = jnp.dot(f, ws, preferred_element_type=F32) + jnp.dot(a, wn, preferred_element_type=F32)
        square = v * v
        tanh = jnp.tanh(root * (v + 0.044715 * (square * v)))
        half = 0.5 * (1.0 + tanh)
        act_ref[...] = (v * half).astype(BF16)
        slope = half + 0.5 * v * (1.0 - tanh * tanh) * (root * (1.0 + 3 * 0.044715 * square))
        g = (go_ref[...].astype(F32) * slope).astype(BF16)
        g_ref[...] = g
        spread = lax.dot_general(g, wn, NT, preferred_element_type=F32).astype(BF16)
        for k, out in enumerate(back):
            out[...] = spread[:, k * width : (k + 1) * width]

    offset = chunk * steps
    in_specs = (
        [pl.BlockSpec((parts, rows, width), lambda i, c: (0, offset + i, 0))]
        + [pl.BlockSpec((rows, width), lambda i, c: (i, 0))] * parts
        + [full(w_self.shape), full(w_neigh.shape)]
        + [pl.BlockSpec((rows, hidden), lambda i, c: (offset + i, 0))]
    )
    args = [col, feat_rows, *agg_parts, w_self, w_neigh, grad_out]
    aliases = {}
    if act_prev is not None:
        in_specs.append(pl.BlockSpec(memory_space=pl.ANY))
        aliases = {len(args): 0}
        args.append(act_prev)
    return pl.pallas_call(
        kernel,
        out_shape=[
            jax.ShapeDtypeStruct((chunk_rows * CHUNKS, hidden), BF16),
            jax.ShapeDtypeStruct((chunk_rows, hidden), BF16),
        ]
        + [jax.ShapeDtypeStruct((chunk_rows, width), BF16)] * parts,
        grid_spec=pltpu.PrefetchScalarGridSpec(
            num_scalar_prefetch=1,
            grid=(steps,),
            in_specs=in_specs,
            out_specs=[
                pl.BlockSpec((rows, hidden), lambda i, c: (offset + i, 0)),
                pl.BlockSpec((rows, hidden), lambda i, c: (i, 0)),
            ]
            + [pl.BlockSpec((rows, width), lambda i, c: (i, 0))] * parts,
        ),
        input_output_aliases=aliases,
        compiler_params=params(),
        name="dense",
    )(*args)


def weights(col, row, feat_rows, agg_chunks, grads, w_self):
    parts, rows, width = feat_rows.shape
    hidden = w_self.shape[1]

    def kernel(col_ref, row_ref, *refs):
        f_ref, refs = refs[0], refs[1:]
        a_refs, refs = refs[: parts * CHUNKS], refs[parts * CHUNKS :]
        g_refs, ws_ref, refs = refs[:CHUNKS], refs[CHUNKS], refs[CHUNKS + 1 :]
        keep_ref, send_ref, s_refs = refs[0], refs[1], refs[2 : 2 + parts]
        agg, spread, sems, out_sems = refs[2 + parts :]
        targets = [
            agg.at[k, h * chunk_rows : (h + 1) * chunk_rows]
            for h in range(CHUNKS)
            for k in range(parts)
        ]
        copies = begin(a_refs, targets, sems)
        g = jnp.concatenate([r[...] for r in g_refs], axis=0)
        ws = permuted(ws_ref, col_ref, parts, width)
        s = lax.dot_general(g, ws, NT, preferred_element_type=F32).astype(BF16)
        for k in range(parts):
            spread[k] = s[:, k * width : (k + 1) * width]
        writes = begin([spread.at[k] for k in range(parts)], s_refs, out_sems)

        def emit(self_ref, neigh_ref):
            for k in range(parts):
                self_ref[k * width : (k + 1) * width, :] = lax.dot_general(
                    f_ref[k], g, TN, preferred_element_type=F32
                )
            for copy in copies:
                copy.wait()
            for k in range(parts):
                neigh_ref[rows_at(k ^ col_ref[0], width), :] = lax.dot_general(
                    agg[k], g, TN, preferred_element_type=F32
                )

        even = row_ref[0] % 2 == 0
        pl.when(even)(lambda: emit(keep_ref, send_ref))
        pl.when(jnp.logical_not(even))(lambda: emit(send_ref, keep_ref))
        for write in writes:
            write.wait()

    flat = [a for chunk in agg_chunks for a in chunk]
    chunk_rows = flat[0].shape[0]
    args = [feat_rows, *flat, *grads, w_self]
    out_shape = [jax.ShapeDtypeStruct((parts * width, hidden), F32)] * 2 + [
        jax.ShapeDtypeStruct((rows, width), BF16)
    ] * parts
    return pl.pallas_call(
        kernel,
        out_shape=out_shape,
        grid_spec=pltpu.PrefetchScalarGridSpec(
            num_scalar_prefetch=2,
            grid=(1,),
            in_specs=[full(feat_rows.shape)]
            + [ANY] * len(flat)
            + [full(a.shape) for a in (*grads, w_self)],
            out_specs=[full(o.shape) for o in out_shape[:2]] + [ANY] * parts,
            scratch_shapes=[
                pltpu.VMEM((parts, rows, width), BF16),
                pltpu.VMEM((parts, rows, width), BF16),
                pltpu.SemaphoreType.DMA((len(flat),)),
                pltpu.SemaphoreType.DMA((parts,)),
            ],
        ),
        compiler_params=params(),
        name="weights",
    )(col, row, *args)


def combine(row, keep, received, chips):
    total, hidden = keep.shape
    rows = total // chips

    def kernel(row_ref, keep_ref, received_ref, *outs):
        for q, out in enumerate(outs):
            at = rows_at((row_ref[0] // 2) ^ q, rows)
            out[...] = keep_ref[at, :] + received_ref[at, :]

    return pl.pallas_call(
        kernel,
        out_shape=[jax.ShapeDtypeStruct((rows, hidden), F32)] * chips,
        grid_spec=pltpu.PrefetchScalarGridSpec(
            num_scalar_prefetch=1,
            grid=(1,),
            in_specs=[full(keep.shape)] * 2,
            out_specs=[full((rows, hidden))] * chips,
        ),
        compiler_params=params(),
        name="combine",
    )(row, keep, received)


def widen(row, mine, other):
    rows, hidden = mine[0].shape
    chips = len(mine)

    def kernel(row_ref, *refs):
        sources, outs = refs[: 2 * chips], refs[2 * chips : 2 * chips + 2]
        pieces, wide, sems, out_sems = refs[2 * chips + 2 :]
        copies = begin(sources, [pieces.at[n] for n in range(2 * chips)], sems)
        even = row_ref[0] % 2 == 0
        writes = []
        for q in range(chips):
            at = rows_at((row_ref[0] // 2) ^ q, rows)
            copies[q].wait()
            copies[chips + q].wait()
            first, second = pieces[q].astype(F32), pieces[chips + q].astype(F32)
            wide[0, q] = jnp.where(even, first, second)
            wide[1, q] = jnp.where(even, second, first)
            for n, out in enumerate(outs):
                writes.append(
                    pltpu.make_async_copy(wide.at[n, q], out.at[at], out_sems.at[n, q])
                )
                writes[-1].start()
        for write in writes:
            write.wait()

    return pl.pallas_call(
        kernel,
        out_shape=[jax.ShapeDtypeStruct((chips * rows, hidden), F32)] * 2,
        grid_spec=pltpu.PrefetchScalarGridSpec(
            num_scalar_prefetch=1,
            grid=(1,),
            in_specs=[ANY] * (2 * chips),
            out_specs=[ANY] * 2,
            scratch_shapes=[
                pltpu.VMEM((2 * chips, rows, hidden), BF16),
                pltpu.VMEM((2, chips, rows, hidden), F32),
                pltpu.SemaphoreType.DMA((2 * chips,)),
                pltpu.SemaphoreType.DMA((2, chips)),
            ],
        ),
        compiler_params=params(),
        name="widen",
    )(row, *mine, *other)


def pull(col, row, colref, grads, adj, partitions, cap, chunk, before):
    blocks, per_block, tile, _ = adj.shape
    parts = len(grads)
    chunk_rows, width = grads[0].shape
    per_part = blocks // parts
    steps = per_part // CHUNKS
    last = chunk == CHUNKS - 1
    pool = blocks + partitions * cap
    extra = [] if before is None else [before]

    def kernel(col_ref, row_ref, colref_ref, *refs):
        g_refs, adj_ref, refs = refs[:parts], refs[parts], refs[parts + 1 :]
        before_ref, outs = refs[: len(extra)], refs[len(extra) : -5]
        grad, acc, held, sems, adj_sems = refs[-5:]

        def first(k):
            return (k ^ col_ref[0]) * per_part + chunk * steps

        def fetch(t, k):
            return pltpu.make_async_copy(
                adj_ref.at[first(k) + t], held.at[t, k], adj_sems.at[t, k]
            )

        sources, targets = list(g_refs), [grad.at[k] for k in range(parts)]
        if extra:
            sources.append(before_ref[0])
            targets.append(acc)
        copies = begin(sources, targets, sems)
        for t in range(steps):
            for k in range(parts):
                fetch(t, k).start()
        if not extra:
            acc[...] = jnp.zeros_like(acc)
        for copy in copies:
            copy.wait()

        @pl.loop(0, steps)
        def _(t):
            for k in range(parts):
                fetch(t, k).wait()
            for k in range(parts):
                b = first(k) + t
                turned = grad[k, rows_at(t, tile), :].T
                for q in range(0, per_block, 2):
                    pair = jnp.concatenate([held[t, k, q], held[t, k, q + 1]], axis=1)
                    both = jnp.dot(turned, pair, preferred_element_type=F32)
                    acc[colref_ref[q, b]] += both[:, :tile]
                    acc[colref_ref[q + 1, b]] += both[:, tile:]

        if last:
            local_ref, remote_ref = outs
            for s in range(blocks):
                local_ref[s * tile : (s + 1) * tile, :] = acc[s].T.astype(BF16)
            for k in range(partitions):
                for s in range(cap):
                    remote_ref[k ^ row_ref[0], s * tile : (s + 1) * tile, :] = (
                        acc[blocks + k * cap + s].T.astype(BF16)
                    )
        else:
            load([acc], [outs[0]], sems)

    if last:
        out_shape = [jax.ShapeDtypeStruct((blocks * tile, width), BF16)]
        out_shape += [jax.ShapeDtypeStruct((partitions, cap * tile, width), BF16)]
        out_specs = [full(o.shape) for o in out_shape]
    else:
        out_shape = [jax.ShapeDtypeStruct((pool, width, tile), F32)]
        out_specs = [ANY]
    return pl.pallas_call(
        kernel,
        out_shape=out_shape,
        grid_spec=pltpu.PrefetchScalarGridSpec(
            num_scalar_prefetch=3,
            grid=(1,),
            in_specs=[ANY] * parts + [ANY] + [ANY] * len(extra),
            out_specs=out_specs,
            scratch_shapes=[
                pltpu.VMEM((parts, chunk_rows, width), BF16),
                pltpu.VMEM((pool, width, tile), F32),
                pltpu.VMEM((steps, parts, per_block, tile, tile), BF16),
                pltpu.SemaphoreType.DMA((parts + 1,)),
                pltpu.SemaphoreType.DMA((steps, parts)),
            ],
        ),
        compiler_params=params(),
        name="pull",
    )(col, row, colref, *grads, adj, *extra)


def finish(col, row, ids, self_parts, local, returned, tile, cap):
    parts = len(self_parts)
    rows, width = self_parts[0].shape
    count = returned.shape[0]

    def kernel(col_ref, row_ref, *refs):
        id_refs, refs = refs[: len(ids)], refs[len(ids) :]
        s_refs, (local_ref, returned_ref, out_ref, own, back, sems) = refs[:parts], refs[parts:]
        load([*s_refs, returned_ref], [*[own.at[k] for k in range(parts)], back], sems)
        where = id_rows(id_refs)
        for k in range(parts):
            at = rows_at(k ^ col_ref[0], rows)
            out_ref[at, :] = own[k].astype(F32) + local_ref[at, :].astype(F32)
        for n in range(1, count):
            ref, j = where[n]
            for s in range(cap):
                target = ref[j, row_ref[0] * cap + s]

                @pl.when(target >= 0)
                def _():
                    out_ref[rows_at(target, tile), :] += back[
                        n ^ row_ref[0], s * tile : (s + 1) * tile, :
                    ].astype(F32)

    return pl.pallas_call(
        kernel,
        out_shape=jax.ShapeDtypeStruct(local.shape, F32),
        grid_spec=pltpu.PrefetchScalarGridSpec(
            num_scalar_prefetch=2,
            grid=(1,),
            in_specs=[SMEM] * len(ids) + [ANY] * parts + [full(local.shape), ANY],
            out_specs=full(local.shape),
            scratch_shapes=[
                pltpu.VMEM((parts, rows, width), BF16),
                pltpu.VMEM(returned.shape, BF16),
                pltpu.SemaphoreType.DMA((parts + 1,)),
            ],
        ),
        compiler_params=params(),
        name="finish",
    )(col, row, *ids, *self_parts, local, returned)


def swap(x, axis, k):
    n = lax.axis_size(axis)
    return lax.ppermute(x, axis, [(i, i ^ k) for i in range(n)])


def exchange(pieces, axis, stride=1):
    out = [pieces[0]]
    for k in range(1, len(pieces)):
        out.append(swap(pieces[k], axis, k * stride))
    return out


def tree_sum(parts):
    while len(parts) > 1:
        parts = [parts[n] + parts[n + 1] for n in range(0, len(parts), 2)]
    return parts[0]


def body(feats, adj_vals, colref, fetch_ids, w_self, w_neigh, grad_out):
    node_rows, width = feats.shape
    blocks, _, tile, _ = adj_vals.shape
    partitions = lax.axis_size("rows")
    parts = lax.axis_size("cols")
    cap = fetch_ids.shape[2]
    chips = partitions // 2
    total_nodes = node_rows * partitions
    row_index, col_index = lax.axis_index("rows"), lax.axis_index("cols")
    col = col_index.astype(jnp.int32).reshape(1)
    row = row_index.astype(jnp.int32).reshape(1)

    feat_rows = lax.all_to_all(
        feats.reshape(parts, node_rows // parts, width), "cols", 0, 0, tiled=True
    )
    known = fetch_ids.reshape(1, partitions * cap)
    known = jnp.pad(known, ((0, 0), (0, -known.shape[1] % 128)))
    ids, hop = [known], 1
    while hop < partitions:
        ids.append(swap(known, "rows", hop))
        known = jnp.concatenate([known, ids[-1]], axis=0)
        hop *= 2
    outgoing = select_tiles(
        row, ids, pltpu.with_memory_space_constraint(feats, pltpu.HBM), tile, cap
    )
    arrived = exchange([None, *outgoing], "rows")[1:]
    pooled = colref.T
    slot = jnp.maximum(pooled - blocks, 0)
    slot = ((slot // cap) ^ row_index) * cap + slot % cap
    places = jnp.where(pooled < blocks, pooled, blocks + slot).astype(jnp.int32)

    adj_vals = pltpu.with_memory_space_constraint(adj_vals, pltpu.HBM)
    agg_chunks, sources = [], [feats, *arrived]
    pool_rows = (blocks + partitions * cap) * tile
    for h in range(CHUNKS):
        pieces = aggregate(col, places, sources, adj_vals, h, parts, pool_rows)
        sources = pieces[parts:] or sources
        agg_chunks.append(exchange(pieces[:parts], "cols"))
    act, grads, grad_chunks = None, [], []
    for h in range(CHUNKS):
        act, g, *back = dense(
            col, feat_rows, agg_chunks[h], w_self, w_neigh, grad_out, act, h
        )
        grads.append(g)
        grad_chunks.append(exchange(back, "cols"))
    keep, send, *self_rows = weights(col, row, feat_rows, agg_chunks, grads, w_self)
    self_parts = exchange(self_rows, "cols")

    received = exchange([keep, send], "rows")[1]
    pieces = combine(row, keep, received, chips)
    partial = tree_sum(exchange(pieces, "rows", 2)).astype(BF16)
    mine = tree_sum([p.astype(F32) for p in exchange([partial] * parts, "cols")])
    mine = (mine * (1.0 / math.sqrt(total_nodes))).astype(BF16)
    pieces = exchange([mine] * chips, "rows", 2)
    other = []
    for piece in pieces:
        other.append(swap(piece, "rows", 1))
    grad_self_w, grad_neigh_w = widen(row, pieces, other)

    before = None
    for h in range(CHUNKS):
        before, *remote = pull(
            col, row, places, grad_chunks[h], adj_vals, partitions, cap, h, before
        )
    returned = lax.all_to_all(remote[0], "rows", 0, 0, tiled=True)
    grad_feats = finish(col, row, ids, self_parts, before, returned, tile, cap)
    return (act, grad_self_w, grad_neigh_w, grad_feats)


def solution(mesh):
    in_specs = (
        P("rows", "cols"),
        P("rows", None, None, None),
        P("rows", None),
        P("rows", None, None),
        P(),
        P(),
        P(("rows", "cols"), None),
    )
    out_specs = (P(("rows", "cols"), None), P(), P(), P("rows", "cols"))
    return jax.shard_map(body, mesh=mesh, in_specs=in_specs, out_specs=out_specs, check_vma=False)
```
